512 devices in a mesh: blk: 16 (over x, z_hi, core), grp: 32 (over y, z_lo).
Axes of the slice: x: 4, y: 4, z: 16 (z_hi: 2, z_lo: 8; z = z_hi * 8 + z_lo), core: 2. Of those that a mesh axis runs over, the one named last changes fastest.
Arguments:
- blocks: float32 [1024, 4, 128, 128], P(('blk', 'grp')), may hold values from -1.5 to 1.5
- columns: int32 [1024, 4], P(('blk', 'grp')), may hold values from -1 to 1023, as said below
- owner_map: int32 [1024], P(('blk', 'grp')), may hold values from 0 to 1023, as said below
- targets: int32 [1024, 4], P(('blk', 'grp')), may hold values from 0 to 1023, as said below
Outputs:
- purified: float32 [1024, 4, 128, 128], P(('blk', 'grp'))
The draws below stay inside these ranges and needn't reach their ends.
Inputs may be any that keep to these rules, and one draw needn't show every extreme that they name: `owner_map`: A permutation of the 1024 block rows; each row's multiply position lies in the same slab, on the same device of grp or on the one next to it; positions ((s * 32 + g) * 2 + i) belong to slab s, device g of grp, slot i. `columns`: live entries of a row are distinct, slot 0 is the row's own multiply position, and every live entry lies on the same grp index as the row's multiply position and at most 2 slabs away from it round the loop; empty slots are -1 and come last. `targets`: entries of a row are distinct, slot 0 is the row itself, all lie on the row's grp index and at most 2 slabs away round the loop.
All inputs are finite; a program needn't handle non-finite values.
Results may differ from the reference program's by a relative error of at most 0.0003.
Values sent between devices are 32-bit elements; how exact they have to be, the bound alone decides.
A program may use at most 64 MiB of HBM per device.

```python
import jax
import jax.numpy as jnp
from jax import lax

BS = 128
R = 2
K = 4
KT = 4
SLABS = 16
GROUP = 32
REACH = 2
NB = 1024


def owner_layout(key):
    base = jax.random.fold_in(key, 101)
    key_upper, key_lower, key_order = jax.random.split(base, 3)
    half_rows = R // 2
    upper_slot = half_rows + jax.random.randint(key_upper, (SLABS, GROUP), 0, half_rows)
    lower_slot = jax.random.randint(key_lower, (SLABS, GROUP), 0, half_rows)
    scores = jax.random.randint(key_order, (SLABS, GROUP, R), 0, 1 << 20) * R + jnp.arange(R, dtype=jnp.int32)
    placed = jnp.argsort(scores, axis=-1).astype(jnp.int32)
    group_at = jnp.arange(GROUP, dtype=jnp.int32)[None, :, None]
    rising = (placed == upper_slot[:, :, None]) & (group_at < GROUP - 1)
    falling = (placed == lower_slot[:, :, None]) & (group_at > 0)
    zero_column = jnp.zeros((SLABS, 1), jnp.int32)
    lower_next = jnp.concatenate([lower_slot[:, 1:], zero_column], axis=1)
    upper_prev = jnp.concatenate([zero_column, upper_slot[:, :-1]], axis=1)
    dest_group = group_at + rising.astype(jnp.int32) - falling.astype(jnp.int32)
    dest_slot = jnp.where(rising, lower_next[:, :, None], jnp.where(falling, upper_prev[:, :, None], placed))
    slab_at = jnp.arange(SLABS, dtype=jnp.int32)[:, None, None]
    return ((slab_at * GROUP + dest_group) * R + dest_slot).reshape(NB).astype(jnp.int32)


def candidates():
    cand_width = (2 * REACH + 1) * R
    candidate = jnp.arange(cand_width, dtype=jnp.int32)
    offset_slab = candidate // R - REACH
    slot_index = candidate % R
    slab_at = jnp.arange(SLABS, dtype=jnp.int32)[:, None, None, None]
    group_at = jnp.arange(GROUP, dtype=jnp.int32)[None, :, None, None]
    cand_ids = (jnp.mod(slab_at + offset_slab, SLABS) * GROUP + group_at) * R + slot_index
    full_ids = jnp.broadcast_to(cand_ids, (SLABS, GROUP, R, cand_width)).astype(jnp.int32)
    own_index = REACH * R + jnp.arange(R, dtype=jnp.int32)[None, None, :, None]
    return (candidate, full_ids, own_index)


def column_pattern(key):
    candidate, full_ids, own_index = candidates()
    cand_width = candidate.shape[0]
    key_pick, key_live = jax.random.split(jax.random.fold_in(key, 202))
    scores = jax.random.randint(key_pick, (SLABS, GROUP, R, cand_width), 0, 1 << 20) * cand_width + candidate
    scores = jnp.where(candidate == own_index, -1, scores)
    chosen = lax.top_k(scores, K - 1)[1]
    picked = jnp.take_along_axis(full_ids, chosen, axis=-1)
    own_ids = jnp.take_along_axis(full_ids, jnp.broadcast_to(own_index, (SLABS, GROUP, R, 1)), axis=-1)
    col_ids = jnp.concatenate([own_ids, picked], axis=-1)
    live_count = K - 2 + jax.random.randint(key_live, (SLABS, GROUP, R, 1), 0, 3)
    dense_slab = jnp.arange(SLABS, dtype=jnp.int32)[:, None, None, None] < max(1, SLABS // 4)
    live_count = jnp.where(dense_slab, K, live_count)
    col_ids = jnp.where(jnp.arange(K, dtype=jnp.int32) < live_count, col_ids, -1)
    return col_ids.reshape(NB, K).astype(jnp.int32)


def draw_owner_map(key, part):
    return owner_layout(key)


def draw_columns(key, part):
    return column_pattern(key)[owner_layout(key)]


def draw_targets(key, part):
    candidate, full_ids, own_index = candidates()
    cand_width = candidate.shape[0]
    key_pick, key_side, key_slot = jax.random.split(jax.random.fold_in(key, 303), 3)
    far_side = jax.random.randint(key_side, (SLABS, GROUP, R, 1), 0, 2) * (2 * REACH)
    far_index = far_side * R + jax.random.randint(key_slot, (SLABS, GROUP, R, 1), 0, R)
    scores = jax.random.randint(key_pick, (SLABS, GROUP, R, cand_width), 0, 1 << 20) * cand_width + candidate
    scores = jnp.where((candidate == own_index) | (candidate == far_index), -1, scores)
    chosen = lax.top_k(scores, KT - 2)[1]
    picked = jnp.take_along_axis(full_ids, chosen, axis=-1)
    own_ids = jnp.take_along_axis(full_ids, jnp.broadcast_to(own_index, (SLABS, GROUP, R, 1)), axis=-1)
    far_ids = jnp.take_along_axis(full_ids, far_index, axis=-1)
    return jnp.concatenate([own_ids, far_ids, picked], axis=-1).reshape(NB, KT).astype(jnp.int32)


def steps_of(rng, shape, pieces, least, top_value):
    level, own = 1.0, jax.random.fold_in(rng, 6)
    for axis_at, parts in pieces:
        steps = jnp.exp(jax.random.uniform(jax.random.fold_in(own, axis_at), (parts,), jnp.float32, least / len(pieces), top_value / len(pieces)))
        level = level * jnp.repeat(steps, shape[axis_at] // parts).reshape([-1 if axis == axis_at else 1 for axis in range(len(shape))])
    return level


def centred(key, dims, deviation, most, cuts=(), kind=jnp.bfloat16):
    drawn = jax.random.normal(key, dims, jnp.float32) * deviation
    if len(cuts) > 0:
        drawn = steps_of(key, dims, cuts, -0.22, 0.18) * drawn
    return jnp.clip(drawn, min=-most, max=most).astype(kind)


def setup_inputs(seed: int = 0) -> dict:
    streams_of = jax.random.split(jax.random.key(seed), 5)
    return {
        "blocks": centred(streams_of[0], (NB, K, BS, BS), 0.25, 1.5, ((0, 512),), jnp.float32),
        "columns": draw_columns(jax.random.fold_in(streams_of[4], 71), 0),
        "owner_map": draw_owner_map(jax.random.fold_in(streams_of[4], 71), 0),
        "targets": draw_targets(jax.random.fold_in(streams_of[4], 71), 0),
    }


FULL_PRECISION = lax.Precision.HIGHEST


def row_terms(left_blocks, left_cols, row_blocks, row_cols, wanted):
    live_mask = (left_cols >= 0).astype(jnp.float32)
    matched = (row_cols[:, None, :] == wanted[None, :, None]).astype(jnp.float32) * live_mask[:, None, None]
    picked = jnp.einsum("abc,acxy->abxy", matched, row_blocks, precision=FULL_PRECISION)
    return jnp.einsum("axz,abzy->bxy", left_blocks, picked, precision=FULL_PRECISION)


def reference(blocks, columns, owner_map, targets):
    matrix = jnp.zeros_like(blocks).at[owner_map].set(blocks)
    pattern = jnp.zeros_like(columns).at[owner_map].set(columns)

    def one_row(position):
        left_cols = pattern[position]
        safe_cols = jnp.maximum(left_cols, 0).astype(jnp.int32)
        wanted = targets[position]
        square_row = row_terms(matrix[position], left_cols, matrix[safe_cols], pattern[safe_cols], wanted)
        cube_row = row_terms(square_row, wanted, matrix[wanted], pattern[wanted], wanted)
        return 3.0 * square_row - 2.0 * cube_row

    return lax.map(one_row, jnp.arange(NB, dtype=jnp.int32))
```

```python
import functools

import jax
import jax.numpy as jnp
from jax import lax
from jax.experimental import pallas as pl
from jax.experimental.pallas import tpu as pltpu
from jax.sharding import PartitionSpec as P

MESH = pl.DeviceIdType.MESH
ROWS, SLOTS, ORDER = 2, 4, 128
CHUNKS = ROWS * SLOTS
Z_LO = 8


def place():
    slab, group = lax.axis_index("blk"), lax.axis_index("grp")
    return slab // 4, (slab // 2) % 2, slab % 2, group // Z_LO, group % Z_LO


def exchange_kernel(
    blocks, pattern, far, far_pattern, mid, mid_pattern, send_sem, recv_sem
):
    x, z_hi, core, y, z_lo = place()
    half = z_lo // 4

    def at(x_, hi_, core_, lo_):
        return ((x_ * 2 + hi_) * 2 + core_, y * Z_LO + lo_)

    up = at(x, (z_hi + half) % 2, core, (z_lo + 4) % Z_LO)
    down = at(x, (z_hi + half + 1) % 2, core, (z_lo + 4) % Z_LO)
    x_to = at((x + 5 - 2 * z_hi) % 4, z_hi, core, z_lo)
    x_from = at((x + 3 + 2 * z_hi) % 4, z_hi, core, z_lo)
    sibling = at(x, z_hi, 1 - core, z_lo)

    barrier = pltpu.get_barrier_semaphore()
    for peer in (up, down, x_to, x_from, sibling):
        pl.semaphore_signal(barrier, inc=1, device_id=peer, device_id_type=MESH)
    pl.semaphore_wait(barrier, 5)

    def copy(stage, i, src, dst, peer):
        return pltpu.make_async_remote_copy(
            src_ref=src,
            dst_ref=dst,
            send_sem=send_sem.at[stage, i],
            recv_sem=recv_sem.at[stage, i],
            device_id=peer,
            device_id_type=MESH,
        )

    pieces = [CHUNKS] + [c for i in range(CHUNKS // 2) for c in (i, i + CHUNKS // 2)]

    def heading(i):
        return up if i < CHUNKS // 2 or i == CHUNKS else down

    def own(i):
        return pattern if i == CHUNKS else blocks.at[i]

    def middle(i):
        return mid_pattern if i == CHUNKS else mid.at[i]

    def slot(k, i):
        return far_pattern.at[k] if i == CHUNKS else far.at[k, i]

    first = {i: copy(0, i, own(i), middle(i), heading(i)) for i in pieces}
    second = {i: copy(1, i, middle(i), slot(0, i), heading(i)) for i in pieces}
    across = {i: copy(2, i, slot(0, i), slot(1, i), x_to) for i in pieces}
    beside = {i: copy(3, i, own(i), slot(2, i), sibling) for i in pieces}
    source = (z_hi + core) % 2
    last = {i: copy(4, i, slot(source, i), slot(3, i), sibling) for i in pieces}

    for i in pieces:
        first[i].start()
    for i in pieces:
        beside[i].start()
    for i in pieces:
        first[i].wait_recv()
        second[i].start()
    for i in pieces:
        second[i].wait_recv()
        across[i].start()
    for i in pieces:
        across[i].wait_recv()
        last[i].start()
    for i in pieces:
        beside[i].wait_recv()
        last[i].wait_recv()
    for stage in (first, second, across, beside, last):
        for i in pieces:
            stage[i].wait_send()


def exchange(blocks, pattern):
    vmem = pl.BlockSpec(memory_space=pltpu.VMEM)
    return pl.pallas_call(
        exchange_kernel,
        out_shape=(
            jax.ShapeDtypeStruct((4, CHUNKS, ORDER, ORDER), jnp.float32),
            jax.ShapeDtypeStruct((4, 8, 128), jnp.int32),
        ),
        in_specs=[vmem, vmem],
        out_specs=(vmem, vmem),
        scratch_shapes=[
            pltpu.VMEM((CHUNKS, ORDER, ORDER), jnp.float32),
            pltpu.VMEM((8, 128), jnp.int32),
            pltpu.SemaphoreType.DMA((5, CHUNKS + 1)),
            pltpu.SemaphoreType.DMA((5, CHUNKS + 1)),
        ],
        compiler_params=pltpu.CompilerParams(collective_id=0, has_side_effects=True),
        name="exchange",
    )(blocks, pattern)


PANEL = 5 * CHUNKS


def split(value):
    high = value.astype(jnp.bfloat16)
    return high, (value - high.astype(jnp.float32)).astype(jnp.bfloat16)


def dot3(left, right_high, right_low):
    high, low = split(left)
    dot = functools.partial(jnp.dot, preferred_element_type=jnp.float32)
    return dot(high, right_high) + (dot(high, right_low) + dot(low, right_high))


def purify_kernel(index, own, far, out, panel_high, panel_low, right_high, right_low):
    def fill(i, value):
        high, low = split(value)
        panel_high[i] = high
        panel_low[i] = low

    for i in range(CHUNKS):
        fill(i, own[i])

    @pl.loop(0, 4 * CHUNKS)
    def _(i):
        fill(CHUNKS + i, far[i])

    panel_high[PANEL] = jnp.zeros((ORDER, ORDER), jnp.bfloat16)
    panel_low[PANEL] = jnp.zeros((ORDER, ORDER), jnp.bfloat16)

    def product(stage, j, left):
        for a in range(SLOTS):
            for b in range(SLOTS):
                at = index[((stage * ROWS + j) * SLOTS + a) * SLOTS + b]
                rows, cols = pl.ds(a * ORDER, ORDER), pl.ds(b * ORDER, ORDER)
                right_high[rows, cols] = panel_high[at]
                right_low[rows, cols] = panel_low[at]
        return dot3(left, right_high[...], right_low[...])

    for j in range(ROWS):
        left = jnp.concatenate([own[j * SLOTS + a] for a in range(SLOTS)], axis=1)
        square = product(0, j, left)
        cube = product(1, j, square)
        result = 3.0 * square - 2.0 * cube
        for b in range(SLOTS):
            out[j, b] = result[:, b * ORDER : (b + 1) * ORDER]


def purify(index, own, far):
    vmem = pl.BlockSpec(memory_space=pltpu.VMEM)
    return pl.pallas_call(
        purify_kernel,
        out_shape=jax.ShapeDtypeStruct((ROWS, SLOTS, ORDER, ORDER), jnp.float32),
        in_specs=[pl.BlockSpec(memory_space=pltpu.SMEM), vmem, vmem],
        out_specs=vmem,
        scratch_shapes=[
            pltpu.VMEM((PANEL + 1, ORDER, ORDER), jnp.bfloat16),
            pltpu.VMEM((PANEL + 1, ORDER, ORDER), jnp.bfloat16),
            pltpu.VMEM((SLOTS * ORDER, SLOTS * ORDER), jnp.bfloat16),
            pltpu.VMEM((SLOTS * ORDER, SLOTS * ORDER), jnp.bfloat16),
        ],
        name="purify",
    )(index, own, far)


def from_neighbours(value, axis):
    peers = lax.axis_size(axis)
    up = [(i, i + 1) for i in range(peers - 1)]
    down = [(i + 1, i) for i in range(peers - 1)]
    return lax.ppermute(value, axis, up), lax.ppermute(value, axis, down)


def per_device(blocks, columns, owner_map, targets):
    group_size, slab_count = lax.axis_size("grp"), lax.axis_size("blk")
    slab, group = lax.axis_index("blk"), lax.axis_index("grp")
    _, z_hi, core, _, _ = place()
    slot_ids = jnp.arange(ROWS, dtype=jnp.int32)

    labels = jnp.concatenate([(owner_map + 1)[:, None], columns], axis=1)
    below, above = from_neighbours(blocks, "grp")
    labels_below, labels_above = from_neighbours(labels, "grp")
    wide_labels = jnp.concatenate([labels_below, labels, labels_above], axis=0)
    own_ids = (slab * group_size + group) * ROWS + slot_ids
    chosen = wide_labels[None, :, 0] == (own_ids + 1)[:, None]
    rows = [value[i] for value in (below, blocks, above) for i in range(ROWS)]
    local = jnp.stack(
        [
            sum(jnp.where(chosen[j, h], rows[h], 0.0) for h in range(3 * ROWS))
            for j in range(ROWS)
        ]
    ).reshape(CHUNKS, ORDER, ORDER)
    local_cols = jnp.sum(
        jnp.where(chosen[:, :, None], wide_labels[None, :, 1:], 0), axis=1
    ).astype(jnp.int32)

    pattern = jnp.pad(local_cols, ((0, 8 - ROWS), (0, 128 - SLOTS)))
    far, far_pattern = exchange(local, pattern)

    two, one = 2 - 4 * z_hi, 1 - 2 * core
    offsets = jnp.stack([jnp.zeros_like(two), two, -two, one, -one])
    ids = (jnp.mod(slab + offsets, slab_count) * group_size + group) * ROWS
    row_ids = (ids[:, None] + slot_ids[None, :]).reshape(-1)
    cols = jnp.concatenate([local_cols[None], far_pattern[:, :ROWS, :SLOTS]], axis=0)
    cols = cols.reshape(PANEL)
    block_rows = jnp.repeat(row_ids, SLOTS)
    left_ids = jnp.stack([local_cols, targets])
    found = (left_ids[:, :, :, None, None] == block_rows) & (
        targets[None, :, None, :, None] == cols
    )
    index = jnp.min(
        jnp.where(found, jnp.arange(PANEL, dtype=jnp.int32), PANEL), axis=-1
    ).reshape(-1)
    return purify(index, local, far.reshape(4 * CHUNKS, ORDER, ORDER))


def solution(mesh):
    return jax.shard_map(
        per_device,
        mesh=mesh,
        in_specs=(
            P(("blk", "grp"), None, None, None),
            P(("blk", "grp"), None),
            P(("blk", "grp")),
            P(("blk", "grp"), None),
        ),
        out_specs=P(("blk", "grp"), None, None, None),
        check_vma=False,
    )
```

```python
import functools

import jax
import jax.numpy as jnp
from jax import lax
from jax.experimental import pallas as pl
from jax.experimental.pallas import tpu as pltpu
from jax.sharding import PartitionSpec as P

MESH = pl.DeviceIdType.MESH
ROWS, SLOTS, ORDER = 2, 4, 128
CHUNKS = ROWS * SLOTS
Z_LO = 8


def place():
    slab, group = lax.axis_index("blk"), lax.axis_index("grp")
    return slab // 4, (slab // 2) % 2, slab % 2, group // Z_LO, group % Z_LO


M1, P1, P7, P9, FC, YN, YF, XC, XB, XA, SC, SB, SA, TC, TB, TA = range(16)
PLACES = 16


def exchange_kernel(blocks, labels, far, far_labels, send_sem, recv_sem):
    x, z_hi, core, y, z_lo = place()
    z = z_hi * Z_LO + z_lo

    def at(x_, z_, core_, y_):
        return ((x_ * 2 + z_ // Z_LO) * 2 + core_, y_ * Z_LO + z_ % Z_LO)

    def along_z(by):
        return at(x, (z + by + 2 * Z_LO) % (2 * Z_LO), core, y)

    inner_low = (z_lo + Z_LO - 1) // Z_LO
    edge_high = (z_lo + 1) // Z_LO
    edge_low = 1 - inner_low
    edge = edge_low + edge_high
    x_to = at((x + 5 - 2 * z_hi) % 4, z, core, y)
    x_from = at((x + 3 + 2 * z_hi) % 4, z, core, y)
    y_to = at(x, z, core, (y + 5 - 2 * edge_high) % 4)
    y_from = at(x, z, core, (y + 3 + 2 * edge_high) % 4)
    sibling = at(x, z, 1 - core, y)
    below, above = P7 + (YF - P7) * edge_low, P9 + (YF - P9) * edge_high

    barrier = pltpu.get_barrier_semaphore()
    peers = [along_z(by) for by in (1, -1, 6, -6)] + [x_to, x_from, y_to, y_from, sibling]
    for peer in peers:
        pl.semaphore_signal(barrier, inc=1, device_id=peer, device_id_type=MESH)
    pl.semaphore_wait(barrier, len(peers))

    def ref(place_, i):
        if place_ is None:
            return labels if i == CHUNKS else blocks.at[i]
        return far_labels.at[place_] if i == CHUNKS else far.at[place_, i]

    def copy(src, dst, i, peer):
        return pltpu.make_async_remote_copy(
            src_ref=ref(src, i),
            dst_ref=ref(dst, i),
            send_sem=send_sem.at[dst, i],
            recv_sem=recv_sem.at[dst, i],
            device_id=peer,
            device_id_type=MESH,
        )

    def send(src, dst, i, peer):
        copy(src, dst, i, peer).start()

    def arrived(dst, i):
        copy(dst, dst, i, sibling).wait_recv()

    def sent(dst, i):
        copy(dst, dst, i, sibling).wait_send()

    pieces = [CHUNKS] + [c for i in range(CHUNKS // 2) for c in (i, i + CHUNKS // 2)]
    upward = {i: i < CHUNKS // 2 or i == CHUNKS for i in pieces}

    for i in pieces:
        send(None, M1 if upward[i] else P1, i, along_z(1 if upward[i] else -1))
    for i in pieces:
        send(None, SC, i, sibling)
    for i in pieces:
        here = M1 if upward[i] else P1
        arrived(here, i)
        send(here, P9 if upward[i] else P7, i, along_z(6 if upward[i] else -6))
        send(None, P1 if upward[i] else M1, i, along_z(-1 if upward[i] else 1))

        @pl.when(edge_low == 1 if upward[i] else edge_high == 1)
        def _():
            send(here, YF, i, y_to)

    for i in pieces:
        here = P1 if upward[i] else M1
        arrived(here, i)

        @pl.when(edge_high == 1 if upward[i] else edge_low == 1)
        def _():
            send(here, YF, i, y_to)

    for i in pieces:
        @pl.when(edge_low == 0)
        def _():
            send(M1, SB, i, sibling)

        @pl.when(edge_high == 0)
        def _():
            send(P1, SA, i, sibling)

    for i in pieces:
        here = P9 if upward[i] else P7
        arrived(here, i)
        send(here, FC, i, along_z(1 if upward[i] else -1))

        @pl.when(edge == 1)
        def _():
            arrived(YF, i)

        if upward[i]:
            send(above, XA, i, x_to)
        else:
            send(below, XB, i, x_to)

        @pl.when(edge_high == 1 if upward[i] else edge_low == 1)
        def _():
            send(here, YN, i, y_to)

    for i in pieces:
        arrived(FC, i)
        send(FC, P7 if upward[i] else P9, i, along_z(1 if upward[i] else -1))
        send(FC, XC, i, x_to)

    crossed = (z_hi + core) % 2
    pass_center = FC + (XC - FC) * crossed
    pass_below = below + (XB - below) * crossed
    pass_above = above + (XA - above) * crossed
    for i in pieces:
        if upward[i]:
            arrived(XA, i)
            send(pass_above, TA, i, sibling)
        else:
            arrived(XB, i)
            send(pass_below, TB, i, sibling)

    for i in pieces:
        here = P7 if upward[i] else P9
        arrived(here, i)
        if upward[i]:
            send(below, XB, i, x_to)
        else:
            send(above, XA, i, x_to)

        @pl.when(edge_low == 1 if upward[i] else edge_high == 1)
        def _():
            send(here, YN, i, y_to)

    for i in pieces:
        arrived(XC, i)
        send(pass_center, TC, i, sibling)

    @pl.when(edge == 1)
    def _():
        for i in pieces:
            arrived(YN, i)

    for i in pieces:
        @pl.when(edge_low == 1)
        def _():
            send(YN, SB, i, sibling)

        @pl.when(edge_high == 1)
        def _():
            send(YN, SA, i, sibling)

    for i in pieces:
        if upward[i]:
            arrived(XB, i)
            send(pass_below, TB, i, sibling)
        else:
            arrived(XA, i)
            send(pass_above, TA, i, sibling)

    always = [p for p in range(PLACES) if p not in (YN, YF)]
    for i in pieces:
        for p in (SC, SB, SA, TC, TB, TA):
            arrived(p, i)
    for i in pieces:
        for p in always:
            sent(p, i)

    @pl.when(edge == 1)
    def _():
        for i in pieces:
            sent(YN, i)
            sent(YF, i)


def exchange(blocks, labels):
    vmem = pl.BlockSpec(memory_space=pltpu.VMEM)
    anywhere = pl.BlockSpec(memory_space=pl.ANY)
    return pl.pallas_call(
        exchange_kernel,
        out_shape=(
            jax.ShapeDtypeStruct((PLACES, CHUNKS, ORDER, ORDER), jnp.float32),
            jax.ShapeDtypeStruct((PLACES, 8, 128), jnp.int32),
        ),
        in_specs=[vmem, vmem],
        out_specs=(anywhere, anywhere),
        scratch_shapes=[
            pltpu.SemaphoreType.DMA((PLACES, CHUNKS + 1)),
            pltpu.SemaphoreType.DMA((PLACES, CHUNKS + 1)),
        ],
        compiler_params=pltpu.CompilerParams(collective_id=0, has_side_effects=True),
        name="exchange",
    )(blocks, labels)


PANEL = (1 + PLACES) * CHUNKS


def split(value):
    high = value.astype(jnp.bfloat16)
    return high, (value - high.astype(jnp.float32)).astype(jnp.bfloat16)


def dot3(left, right_high, right_low):
    high, low = split(left)
    dot = functools.partial(jnp.dot, preferred_element_type=jnp.float32)
    return dot(high, right_high) + (dot(high, right_low) + dot(low, right_high))


def purify_kernel(index, own, far, out, panel, right_high, right_low, sem):
    fetched = [
        pltpu.make_async_copy(far, panel.at[pl.ds(CHUNKS, PLACES * CHUNKS)], sem.at[0]),
        pltpu.make_async_copy(own, panel.at[pl.ds(0, CHUNKS)], sem.at[1]),
    ]
    for copy in fetched:
        copy.start()
    panel[PANEL] = jnp.zeros((ORDER, ORDER), jnp.float32)
    for copy in fetched:
        copy.wait()

    def product(stage, j, left):
        for a in range(SLOTS):
            for b in range(SLOTS):
                at = index[CHUNKS + ((stage * ROWS + j) * SLOTS + a) * SLOTS + b]
                rows, cols = pl.ds(a * ORDER, ORDER), pl.ds(b * ORDER, ORDER)
                high, low = split(panel[at])
                right_high[rows, cols] = high
                right_low[rows, cols] = low
        return dot3(left, right_high[...], right_low[...])

    for j in range(ROWS):
        left = jnp.concatenate([panel[index[j * SLOTS + a]] for a in range(SLOTS)], axis=1)
        square = product(0, j, left)
        cube = product(1, j, square)
        result = 3.0 * square - 2.0 * cube
        for b in range(SLOTS):
            out[j, b] = result[:, b * ORDER : (b + 1) * ORDER]


def purify(index, own, far):
    vmem = pl.BlockSpec(memory_space=pltpu.VMEM)
    anywhere = pl.BlockSpec(memory_space=pl.ANY)
    return pl.pallas_call(
        purify_kernel,
        out_shape=jax.ShapeDtypeStruct((ROWS, SLOTS, ORDER, ORDER), jnp.float32),
        in_specs=[pl.BlockSpec(memory_space=pltpu.SMEM), anywhere, anywhere],
        out_specs=vmem,
        scratch_shapes=[
            pltpu.VMEM((PANEL + 1, ORDER, ORDER), jnp.float32),
            pltpu.VMEM((SLOTS * ORDER, SLOTS * ORDER), jnp.bfloat16),
            pltpu.VMEM((SLOTS * ORDER, SLOTS * ORDER), jnp.bfloat16),
            pltpu.SemaphoreType.DMA((2,)),
        ],
        name="purify",
    )(index, own, far)


def per_device(blocks, columns, owner_map, targets):
    group_size = lax.axis_size("grp")
    slab, group = lax.axis_index("blk"), lax.axis_index("grp")
    _, _, _, _, z_lo = place()
    blocks = blocks.reshape(CHUNKS, ORDER, ORDER)
    labels = jnp.pad(
        jnp.concatenate([owner_map[:, None], columns], axis=1),
        ((0, 8 - ROWS), (0, 128 - SLOTS - 1)),
    )
    far, far_labels = exchange(blocks, labels)

    tiles = jnp.concatenate([labels[None], far_labels], axis=0)[:, :ROWS, : SLOTS + 1]
    tile = jnp.arange(1 + PLACES, dtype=jnp.int32)[:, None]
    unused = ((tile == 1 + YN) | (tile == 1 + YF)) & (z_lo > 0) & (z_lo < Z_LO - 1)
    owners = jnp.where(unused, -2, tiles[:, :, 0]).reshape(-1)
    cols = tiles[:, :, 1:].reshape(-1, SLOTS)
    own_ids = (slab * group_size + group) * ROWS + jnp.arange(ROWS, dtype=jnp.int32)
    mine = owners[None, :] == own_ids[:, None]
    local_cols = jnp.sum(jnp.where(mine[:, :, None], cols[None], 0), axis=1)
    first = jnp.arange(owners.shape[0], dtype=jnp.int32) * SLOTS
    left = jnp.sum(jnp.where(mine, first[None], 0), axis=1)[:, None]
    left = left + jnp.arange(SLOTS, dtype=jnp.int32)[None]

    left_ids = jnp.stack([local_cols, targets])
    found = (left_ids[:, :, :, None, None] == jnp.repeat(owners, SLOTS)) & (
        targets[None, :, None, :, None] == cols.reshape(-1)
    )
    right = jnp.min(jnp.where(found, jnp.arange(PANEL, dtype=jnp.int32), PANEL), axis=-1)
    index = jnp.concatenate([left.reshape(-1), right.reshape(-1)])
    return purify(index, blocks, far.reshape(PLACES * CHUNKS, ORDER, ORDER))


def solution(mesh):
    return jax.shard_map(
        per_device,
        mesh=mesh,
        in_specs=(
            P(("blk", "grp"), None, None, None),
            P(("blk", "grp"), None),
            P(("blk", "grp")),
            P(("blk", "grp"), None),
        ),
        out_specs=P(("blk", "grp"), None, None, None),
        check_vma=False,
    )
```

```python
import functools

import jax
import jax.numpy as jnp
from jax import lax
from jax.experimental import pallas as pl
from jax.experimental.pallas import tpu as pltpu
from jax.sharding import PartitionSpec as P

MESH = pl.DeviceIdType.MESH
ROWS, SLOTS, ORDER = 2, 4, 128
CHUNKS = ROWS * SLOTS
Z_LO = 8


def place():
    slab, group = lax.axis_index("blk"), lax.axis_index("grp")
    return slab // 4, (slab // 2) % 2, slab % 2, group // Z_LO, group % Z_LO


M1, P1, P7, P9, FC, YN, YF, XC, XB, XA, SC, SB, SA, TC, TB, TA = range(16)
PLACES = 16


PANEL = (PLACES + 1) * CHUNKS
QUERIES = 2 * ROWS * SLOTS * SLOTS


def find(queries, known, index):
    owners = known[:, :CHUNKS, :].reshape(PANEL, 128)
    cols = known[:, CHUNKS:, :].reshape(PANEL, 128)
    at = lax.broadcasted_iota(jnp.int32, (PANEL, 128), 0)
    row, slot, wanted, target_row, stage = [queries[i : i + 1, :] for i in range(5)]
    mine = (owners == row) & (at % SLOTS == slot)
    left = jnp.min(jnp.where(mine, at, PANEL), axis=0, keepdims=True)
    column = jnp.sum(jnp.where(mine, cols, 0), axis=0, keepdims=True)
    middle = jnp.where(stage == 1, target_row, column)
    found = (owners == middle) & (cols == wanted)
    right = jnp.min(jnp.where(found, at, PANEL), axis=0, keepdims=True)
    lane = lax.broadcasted_iota(jnp.int32, (1, 128), 1)

    def scalar(vector, q):
        return jnp.sum(jnp.where(lane == q, vector, 0))

    for j in range(ROWS):
        for a in range(SLOTS):
            index[j * SLOTS + a] = scalar(left, (j * SLOTS + a) * SLOTS)
    for q in range(QUERIES):
        index[CHUNKS + q] = scalar(right, q)


def split(value):
    high = value.astype(jnp.bfloat16)
    return high, (value - high.astype(jnp.float32)).astype(jnp.bfloat16)


def dot3(left, right_high, right_low):
    high, low = split(left)
    dot = functools.partial(jnp.dot, preferred_element_type=jnp.float32)
    return dot(high, right_high) + (dot(high, right_low) + dot(low, right_high))


def kernel(
    queries, blocks, labels, out, panel, known, right_high, right_low, index, send_sem, recv_sem
):
    x, z_hi, core, y, z_lo = place()
    z = z_hi * Z_LO + z_lo

    def at(x_, z_, core_, y_):
        return ((x_ * 2 + z_ // Z_LO) * 2 + core_, y_ * Z_LO + z_ % Z_LO)

    def along_z(by):
        return at(x, (z + by + 2 * Z_LO) % (2 * Z_LO), core, y)

    inner_low = (z_lo + Z_LO - 1) // Z_LO
    edge_high = (z_lo + 1) // Z_LO
    edge_low = 1 - inner_low
    edge = edge_low + edge_high
    x_to = at((x + 5 - 2 * z_hi) % 4, z, core, y)
    x_from = at((x + 3 + 2 * z_hi) % 4, z, core, y)
    y_to = at(x, z, core, (y + 5 - 2 * edge_high) % 4)
    y_from = at(x, z, core, (y + 3 + 2 * edge_high) % 4)
    sibling = at(x, z, 1 - core, y)
    below, above = P7 + (YF - P7) * edge_low, P9 + (YF - P9) * edge_high

    for p in (YN, YF):
        known[p] = jnp.full(known.shape[1:], -2, jnp.int32)

    barrier = pltpu.get_barrier_semaphore()
    peers = [along_z(by) for by in (1, -1, 6, -6)] + [x_to, x_from, y_to, y_from, sibling]
    for peer in peers:
        pl.semaphore_signal(barrier, inc=1, device_id=peer, device_id_type=MESH)
    pl.semaphore_wait(barrier, len(peers))

    def ref(place_, i):
        if place_ is None:
            return labels if i == CHUNKS else blocks.at[i]
        return known.at[place_] if i == CHUNKS else panel.at[place_ * CHUNKS + i]

    def copy(src, dst, i, peer):
        return pltpu.make_async_remote_copy(
            src_ref=ref(src, i),
            dst_ref=ref(dst, i),
            send_sem=send_sem.at[dst, i],
            recv_sem=recv_sem.at[dst, i],
            device_id=peer,
            device_id_type=MESH,
        )

    def send(src, dst, i, peer):
        copy(src, dst, i, peer).start()

    def arrived(dst, i):
        copy(dst, dst, i, sibling).wait_recv()

    def sent(dst, i):
        copy(dst, dst, i, sibling).wait_send()

    half = CHUNKS // 2
    pieces = list(range(CHUNKS + 1))
    upward = {i: i < half or i == CHUNKS for i in pieces}

    def of(k):
        return ([CHUNKS] if k == 0 else []) + [k, k + half]

    def start(k):
        for i in of(k):
            send(None, M1 if upward[i] else P1, i, along_z(1 if upward[i] else -1))

    def six_on(k):
        for i in of(k):
            here = M1 if upward[i] else P1
            arrived(here, i)
            send(None, P1 if upward[i] else M1, i, along_z(-1 if upward[i] else 1))
            send(here, P9 if upward[i] else P7, i, along_z(6 if upward[i] else -6))

            @pl.when(edge_low == 1 if upward[i] else edge_high == 1)
            def _():
                send(here, YF, i, y_to)

    def other_way(k):
        for i in of(k):
            here = P1 if upward[i] else M1
            arrived(here, i)

            @pl.when(edge_high == 1 if upward[i] else edge_low == 1)
            def _():
                send(here, YF, i, y_to)

    def near():
        for i in pieces:
            @pl.when(edge_low == 0)
            def _():
                send(M1, SB, i, sibling)

            @pl.when(edge_high == 0)
            def _():
                send(P1, SA, i, sibling)

    def to_far(k):
        for i in of(k):
            here = P9 if upward[i] else P7
            arrived(here, i)
            send(here, FC, i, along_z(1 if upward[i] else -1))

            @pl.when(edge_high == 1 if upward[i] else edge_low == 1)
            def _():
                send(here, YN, i, y_to)

    def cross(k):
        for i in of(k):
            @pl.when(edge == 1)
            def _():
                arrived(YF, i)

            if upward[i]:
                send(above, XA, i, x_to)
            else:
                send(below, XB, i, x_to)

    def past_far(k):
        for i in of(k):
            arrived(FC, i)
            send(FC, P7 if upward[i] else P9, i, along_z(1 if upward[i] else -1))
            send(FC, XC, i, x_to)

    def end(k):
        for i in of(k):
            here = P7 if upward[i] else P9
            arrived(here, i)
            if upward[i]:
                send(below, XB, i, x_to)
            else:
                send(above, XA, i, x_to)

            @pl.when(edge_low == 1 if upward[i] else edge_high == 1)
            def _():
                send(here, YN, i, y_to)

    crossed = (z_hi + core) % 2
    pass_center = FC + (XC - FC) * crossed
    pass_below = below + (XB - below) * crossed
    pass_above = above + (XA - above) * crossed

    def pass_on(k, early):
        for i in of(k):
            if upward[i] == early:
                arrived(XA, i)
                send(pass_above, TA, i, sibling)
            else:
                arrived(XB, i)
                send(pass_below, TB, i, sibling)

    def pass_far(k):
        for i in of(k):
            arrived(XC, i)
            send(pass_center, TC, i, sibling)

    def near_end(which):
        @pl.when(edge_low == 1)
        def _():
            for i in which:
                arrived(YN, i)
                send(YN, SB, i, sibling)

        @pl.when(edge_high == 1)
        def _():
            for i in which:
                arrived(YN, i)
                send(YN, SA, i, sibling)

    for k in range(half):
        start(k)
    for i in [CHUNKS] + pieces[:-1]:
        send(None, SC, i, sibling)
    own = PLACES * CHUNKS
    for i in range(CHUNKS):
        panel[own + i] = blocks[i]
    panel[PANEL] = jnp.zeros((ORDER, ORDER), jnp.float32)
    known[PLACES] = labels[...]

    six_on(0), six_on(1)
    other_way(0), to_far(0), six_on(2), cross(0)
    other_way(1), to_far(1), six_on(3), past_far(0), cross(1)
    other_way(2), to_far(2), past_far(1), end(0), cross(2)
    other_way(3), near()
    pass_on(0, True), pass_on(1, True)
    to_far(3), past_far(2), end(1), cross(3)
    pass_far(0), pass_on(2, True), pass_on(0, False), near_end([CHUNKS])
    past_far(3), end(2)
    pass_far(1), pass_far(2), pass_on(3, True), pass_on(1, False)
    end(3)
    near_end(pieces[:-1])

    core_places = (SC, SB, SA, TC, TB, TA)
    for p in core_places:
        arrived(p, CHUNKS)
    find(queries, known, index)

    pass_on(2, False), pass_far(3), pass_on(3, False)
    for i in pieces[:-1]:
        for p in core_places:
            arrived(p, i)

    def product(stage, j, left):
        for a in range(SLOTS):
            for b in range(SLOTS):
                at_ = index[CHUNKS + ((stage * ROWS + j) * SLOTS + a) * SLOTS + b]
                rows, cols = pl.ds(a * ORDER, ORDER), pl.ds(b * ORDER, ORDER)
                high, low = split(panel[at_])
                right_high[rows, cols] = high
                right_low[rows, cols] = low
        return dot3(left, right_high[...], right_low[...])

    for j in range(ROWS):
        left = jnp.concatenate([panel[index[j * SLOTS + a]] for a in range(SLOTS)], axis=1)
        square = product(0, j, left)
        cube = product(1, j, square)
        result = 3.0 * square - 2.0 * cube
        for b in range(SLOTS):
            out[j, b] = result[:, b * ORDER : (b + 1) * ORDER]

    always = [p for p in range(PLACES) if p not in (YN, YF)]
    for i in pieces:
        for p in always:
            sent(p, i)

    @pl.when(edge == 1)
    def _():
        for i in pieces:
            sent(YN, i)
            sent(YF, i)


def per_device(blocks, columns, owner_map, targets):
    slab, group = lax.axis_index("blk"), lax.axis_index("grp")
    first_row = (slab * lax.axis_size("grp") + group) * ROWS

    def lanes(values):
        return jnp.broadcast_to(values.reshape(-1, 1), (CHUNKS, 128))

    labels = jnp.concatenate([lanes(jnp.repeat(owner_map, SLOTS)), lanes(columns)], axis=0)
    shape = (2, ROWS, SLOTS, SLOTS)
    stage, row, slot, _ = [lax.broadcasted_iota(jnp.int32, shape, i) for i in range(4)]
    queries = jnp.stack(
        [
            first_row + row,
            slot,
            jnp.broadcast_to(targets[None, :, None, :], shape),
            jnp.broadcast_to(targets[None, :, :, None], shape),
            stage,
        ]
    ).reshape(5, QUERIES)
    queries = jnp.pad(queries, ((0, 3), (0, 128 - QUERIES)), constant_values=-3)
    vmem = pl.BlockSpec(memory_space=pltpu.VMEM)
    return pl.pallas_call(
        kernel,
        out_shape=jax.ShapeDtypeStruct((ROWS, SLOTS, ORDER, ORDER), jnp.float32),
        in_specs=[vmem, vmem, vmem],
        out_specs=vmem,
        scratch_shapes=[
            pltpu.VMEM((PANEL + 1, ORDER, ORDER), jnp.float32),
            pltpu.VMEM((PLACES + 1, 2 * CHUNKS, 128), jnp.int32),
            pltpu.VMEM((SLOTS * ORDER, SLOTS * ORDER), jnp.bfloat16),
            pltpu.VMEM((SLOTS * ORDER, SLOTS * ORDER), jnp.bfloat16),
            pltpu.SMEM((CHUNKS + QUERIES,), jnp.int32),
            pltpu.SemaphoreType.DMA((PLACES, CHUNKS + 1)),
            pltpu.SemaphoreType.DMA((PLACES, CHUNKS + 1)),
        ],
        compiler_params=pltpu.CompilerParams(collective_id=0, has_side_effects=True),
        name="purify",
    )(queries, blocks.reshape(CHUNKS, ORDER, ORDER), labels)


def solution(mesh):
    return jax.shard_map(
        per_device,
        mesh=mesh,
        in_specs=(
            P(("blk", "grp"), None, None, None),
            P(("blk", "grp"), None),
            P(("blk", "grp")),
            P(("blk", "grp"), None),
        ),
        out_specs=P(("blk", "grp"), None, None, None),
        check_vma=False,
    )
```

```python
import functools

import jax
import jax.numpy as jnp
from jax import lax
from jax.experimental import pallas as pl
from jax.experimental.pallas import tpu as pltpu
from jax.sharding import PartitionSpec as P

MESH = pl.DeviceIdType.MESH
ROWS, SLOTS, ORDER = 2, 4, 128
CHUNKS = ROWS * SLOTS
PARTS = 2
PIECES = CHUNKS * PARTS
AHEAD = 2
Z_LO = 8


def place():
    slab, group = lax.axis_index("blk"), lax.axis_index("grp")
    return slab // 4, (slab // 2) % 2, slab % 2, group // Z_LO, group % Z_LO


M1, P1, P7, P9, FC, YN, YF, XC, XB, XA, SC, SB, SA, TC, TB, TA = range(16)
PLACES = 16


PANEL = (PLACES + 1) * CHUNKS
QUERIES = 2 * ROWS * SLOTS * SLOTS


def find(queries, known, index):
    owners = known[:, :CHUNKS, :].reshape(PANEL, 128)
    cols = known[:, CHUNKS:, :].reshape(PANEL, 128)
    at = lax.broadcasted_iota(jnp.int32, (PANEL, 128), 0)
    row, slot, wanted, target_row, stage = [queries[i : i + 1, :] for i in range(5)]
    mine = (owners == row) & (at % SLOTS == slot)
    left = jnp.min(jnp.where(mine, at, PANEL), axis=0, keepdims=True)
    column = jnp.sum(jnp.where(mine, cols, 0), axis=0, keepdims=True)
    middle = jnp.where(stage == 1, target_row, column)
    found = (owners == middle) & (cols == wanted)
    right = jnp.min(jnp.where(found, at, PANEL), axis=0, keepdims=True)
    lane = lax.broadcasted_iota(jnp.int32, (1, 128), 1)

    def scalar(vector, q):
        return jnp.sum(jnp.where(lane == q, vector, 0))

    for j in range(ROWS):
        for a in range(SLOTS):
            index[j * SLOTS + a] = scalar(left, (j * SLOTS + a) * SLOTS)
    for q in range(QUERIES):
        index[CHUNKS + q] = scalar(right, q)


def split(value):
    high = value.astype(jnp.bfloat16)
    return high, (value - high.astype(jnp.float32)).astype(jnp.bfloat16)


def dot3(left, right_high, right_low):
    high, low = split(left)
    dot = functools.partial(jnp.dot, preferred_element_type=jnp.float32)
    return dot(high, right_high) + (dot(high, right_low) + dot(low, right_high))


def kernel(
    queries, blocks, labels, out, panel, known, right_high, right_low, index, send_sem, recv_sem
):
    x, z_hi, core, y, z_lo = place()
    z = z_hi * Z_LO + z_lo

    def at(x_, z_, core_, y_):
        return ((x_ * 2 + z_ // Z_LO) * 2 + core_, y_ * Z_LO + z_ % Z_LO)

    def along_z(by):
        return at(x, (z + by + 2 * Z_LO) % (2 * Z_LO), core, y)

    inner_low = (z_lo + Z_LO - 1) // Z_LO
    edge_high = (z_lo + 1) // Z_LO
    edge_low = 1 - inner_low
    edge = edge_low + edge_high
    x_to = at((x + 5 - 2 * z_hi) % 4, z, core, y)
    x_from = at((x + 3 + 2 * z_hi) % 4, z, core, y)
    y_to = at(x, z, core, (y + 5 - 2 * edge_high) % 4)
    y_from = at(x, z, core, (y + 3 + 2 * edge_high) % 4)
    sibling = at(x, z, 1 - core, y)
    below, above = P7 + (YF - P7) * edge_low, P9 + (YF - P9) * edge_high

    for p in (YN, YF):
        known[p] = jnp.full(known.shape[1:], -2, jnp.int32)

    barrier = pltpu.get_barrier_semaphore()
    peers = [along_z(by) for by in (1, -1, 6, -6)] + [x_to, x_from, y_to, y_from, sibling]
    for peer in peers:
        pl.semaphore_signal(barrier, inc=1, device_id=peer, device_id_type=MESH)
    pl.semaphore_wait(barrier, len(peers))

    def part(i):
        return pl.ds(i % PARTS * (ORDER // PARTS), ORDER // PARTS)

    def ref(place_, i):
        if place_ is None:
            return labels if i == PIECES else blocks.at[i // PARTS, part(i)]
        return known.at[place_] if i == PIECES else panel.at[place_ * CHUNKS + i // PARTS, part(i)]

    def copy(src, dst, i, peer):
        return pltpu.make_async_remote_copy(
            src_ref=ref(src, i),
            dst_ref=ref(dst, i),
            send_sem=send_sem.at[dst, i],
            recv_sem=recv_sem.at[dst, i],
            device_id=peer,
            device_id_type=MESH,
        )

    def send(src, dst, i, peer):
        copy(src, dst, i, peer).start()

    def arrived(dst, i):
        copy(dst, dst, i, sibling).wait_recv()

    def sent(dst, i):
        copy(dst, dst, i, sibling).wait_send()

    steps = PIECES // 2
    pieces = list(range(PIECES + 1))
    upward = {i: i < steps or i == PIECES for i in pieces}

    def of(k):
        return ([PIECES] if k == 0 else []) + [k, k + steps]

    def start(k):
        for i in of(k):
            send(None, M1 if upward[i] else P1, i, along_z(1 if upward[i] else -1))

    def six_on(k):
        for i in of(k):
            here = M1 if upward[i] else P1
            arrived(here, i)
            send(None, P1 if upward[i] else M1, i, along_z(-1 if upward[i] else 1))
            send(here, P9 if upward[i] else P7, i, along_z(6 if upward[i] else -6))

            @pl.when(edge_low == 1 if upward[i] else edge_high == 1)
            def _():
                send(here, YF, i, y_to)

    def other_way(k):
        for i in of(k):
            here = P1 if upward[i] else M1
            arrived(here, i)

            @pl.when(edge_high == 1 if upward[i] else edge_low == 1)
            def _():
                send(here, YF, i, y_to)

    def near(k):
        for i in of(k):
            @pl.when(edge_low == 0)
            def _():
                send(M1, SB, i, sibling)

            @pl.when(edge_high == 0)
            def _():
                send(P1, SA, i, sibling)

    def to_far(k):
        for i in of(k):
            here = P9 if upward[i] else P7
            arrived(here, i)
            send(here, FC, i, along_z(1 if upward[i] else -1))

            @pl.when(edge_high == 1 if upward[i] else edge_low == 1)
            def _():
                send(here, YN, i, y_to)

    def cross(k):
        for i in of(k):
            @pl.when(edge == 1)
            def _():
                arrived(YF, i)

            if upward[i]:
                send(above, XA, i, x_to)
            else:
                send(below, XB, i, x_to)

    def past_far(k):
        for i in of(k):
            arrived(FC, i)
            send(FC, P7 if upward[i] else P9, i, along_z(1 if upward[i] else -1))
            send(FC, XC, i, x_to)

    def end(k):
        for i in of(k):
            here = P7 if upward[i] else P9
            arrived(here, i)
            if upward[i]:
                send(below, XB, i, x_to)
            else:
                send(above, XA, i, x_to)

            @pl.when(edge_low == 1 if upward[i] else edge_high == 1)
            def _():
                send(here, YN, i, y_to)

    crossed = (z_hi + core) % 2
    pass_center = FC + (XC - FC) * crossed
    pass_below = below + (XB - below) * crossed
    pass_above = above + (XA - above) * crossed

    def pass_on(k, early):
        for i in of(k):
            if upward[i] == early:
                arrived(XA, i)
                send(pass_above, TA, i, sibling)
            else:
                arrived(XB, i)
                send(pass_below, TB, i, sibling)

    def pass_far(k):
        for i in of(k):
            arrived(XC, i)
            send(pass_center, TC, i, sibling)

    def near_end(which):
        @pl.when(edge_low == 1)
        def _():
            for i in which:
                arrived(YN, i)
                send(YN, SB, i, sibling)

        @pl.when(edge_high == 1)
        def _():
            for i in which:
                arrived(YN, i)
                send(YN, SA, i, sibling)

    for k in range(steps):
        start(k)
    for k in range(steps):
        for i in of(k):
            send(None, SC, i, sibling)
    own = PLACES * CHUNKS
    for i in range(CHUNKS):
        panel[own + i] = blocks[i]
    panel[PANEL] = jnp.zeros((ORDER, ORDER), jnp.float32)
    known[PLACES] = labels[...]

    def at_step(k, work):
        if 0 <= k < steps:
            work(k)

    core_places = (SC, SB, SA, TC, TB, TA)
    for k in range(AHEAD):
        six_on(k)
    for k in range(steps + 4):
        at_step(k, other_way)
        at_step(k, to_far)
        at_step(k + AHEAD, six_on)
        at_step(k - 1, past_far)
        at_step(k, cross)
        at_step(k - 2, end)
        at_step(k, near)
        at_step(k - 2, lambda k: pass_on(k, True))
        at_step(k - 3, pass_far)
        at_step(k - 4, lambda k: near_end(of(k)))
        at_step(k - 4, lambda k: pass_on(k, False))
        if k == steps + 1:
            for p in core_places:
                arrived(p, PIECES)
            find(queries, known, index)
    for i in pieces[:-1]:
        for p in core_places:
            arrived(p, i)

    def product(stage, j, left):
        for a in range(SLOTS):
            for b in range(SLOTS):
                at_ = index[CHUNKS + ((stage * ROWS + j) * SLOTS + a) * SLOTS + b]
                rows, cols = pl.ds(a * ORDER, ORDER), pl.ds(b * ORDER, ORDER)
                high, low = split(panel[at_])
                right_high[rows, cols] = high
                right_low[rows, cols] = low
        return dot3(left, right_high[...], right_low[...])

    for j in range(ROWS):
        left = jnp.concatenate([panel[index[j * SLOTS + a]] for a in range(SLOTS)], axis=1)
        square = product(0, j, left)
        cube = product(1, j, square)
        result = 3.0 * square - 2.0 * cube
        for b in range(SLOTS):
            out[j, b] = result[:, b * ORDER : (b + 1) * ORDER]

    always = [p for p in range(PLACES) if p not in (YN, YF)]
    for i in pieces:
        for p in always:
            sent(p, i)

    @pl.when(edge == 1)
    def _():
        for i in pieces:
            sent(YN, i)
            sent(YF, i)


def per_device(blocks, columns, owner_map, targets):
    slab, group = lax.axis_index("blk"), lax.axis_index("grp")
    first_row = (slab * lax.axis_size("grp") + group) * ROWS

    def lanes(values):
        return jnp.broadcast_to(values.reshape(-1, 1), (CHUNKS, 128))

    labels = jnp.concatenate([lanes(jnp.repeat(owner_map, SLOTS)), lanes(columns)], axis=0)
    shape = (2, ROWS, SLOTS, SLOTS)
    stage, row, slot, _ = [lax.broadcasted_iota(jnp.int32, shape, i) for i in range(4)]
    queries = jnp.stack(
        [
            first_row + row,
            slot,
            jnp.broadcast_to(targets[None, :, None, :], shape),
            jnp.broadcast_to(targets[None, :, :, None], shape),
            stage,
        ]
    ).reshape(5, QUERIES)
    queries = jnp.pad(queries, ((0, 3), (0, 128 - QUERIES)), constant_values=-3)
    vmem = pl.BlockSpec(memory_space=pltpu.VMEM)
    return pl.pallas_call(
        kernel,
        out_shape=jax.ShapeDtypeStruct((ROWS, SLOTS, ORDER, ORDER), jnp.float32),
        in_specs=[vmem, vmem, vmem],
        out_specs=vmem,
        scratch_shapes=[
            pltpu.VMEM((PANEL + 1, ORDER, ORDER), jnp.float32),
            pltpu.VMEM((PLACES + 1, 2 * CHUNKS, 128), jnp.int32),
            pltpu.VMEM((SLOTS * ORDER, SLOTS * ORDER), jnp.bfloat16),
            pltpu.VMEM((SLOTS * ORDER, SLOTS * ORDER), jnp.bfloat16),
            pltpu.SMEM((CHUNKS + QUERIES,), jnp.int32),
            pltpu.SemaphoreType.DMA((PLACES, PIECES + 1)),
            pltpu.SemaphoreType.DMA((PLACES, PIECES + 1)),
        ],
        compiler_params=pltpu.CompilerParams(collective_id=0, has_side_effects=True),
        name="purify",
    )(queries, blocks.reshape(CHUNKS, ORDER, ORDER), labels)


def solution(mesh):
    return jax.shard_map(
        per_device,
        mesh=mesh,
        in_specs=(
            P(("blk", "grp"), None, None, None),
            P(("blk", "grp"), None),
            P(("blk", "grp")),
            P(("blk", "grp"), None),
        ),
        out_specs=P(("blk", "grp"), None, None, None),
        check_vma=False,
    )
```

```python
import functools

import jax
import jax.numpy as jnp
from jax import lax
from jax.experimental import pallas as pl
from jax.experimental.pallas import tpu as pltpu
from jax.sharding import PartitionSpec as P

MESH = pl.DeviceIdType.MESH
ROWS, SLOTS, ORDER = 2, 4, 128
CHUNKS = ROWS * SLOTS
PARTS = 2
PIECES = CHUNKS * PARTS
AHEAD = 2
Z_LO = 8


def place():
    slab, group = lax.axis_index("blk"), lax.axis_index("grp")
    return slab // 4, (slab // 2) % 2, slab % 2, group // Z_LO, group % Z_LO


M1, P1, P7, P9, FC, YN, YF, XC, XB, XA, SC, SB, SA, TC, TB, TA = range(16)
PLACES = 16


PANEL = (PLACES + 1) * CHUNKS
QUERIES = 2 * ROWS * SLOTS * SLOTS


def find(targets, known, index):
    owners = known[:, :CHUNKS, :].reshape(PANEL, 128)
    cols = known[:, CHUNKS:, :].reshape(PANEL, 128)
    at = lax.broadcasted_iota(jnp.int32, (PANEL, 128), 0)
    lane = lax.broadcasted_iota(jnp.int32, (1, 128), 1)
    slot, b = lane // SLOTS % SLOTS, lane % SLOTS
    j, stage = lane // SLOTS**2 % ROWS, lane // (SLOTS**2 * ROWS)
    first = (lax.axis_index("blk") * lax.axis_size("grp") + lax.axis_index("grp")) * ROWS
    row = first + j
    wanted = target_row = jnp.full((1, 128), -3, jnp.int32)
    for r in range(ROWS):
        for t in range(SLOTS):
            wanted = jnp.where((j == r) & (b == t), targets[r, t], wanted)
            target_row = jnp.where((j == r) & (slot == t), targets[r, t], target_row)
    mine = (owners == row) & (at % SLOTS == slot)
    left = jnp.min(jnp.where(mine, at, PANEL), axis=0, keepdims=True)
    column = jnp.sum(jnp.where(mine, cols, 0), axis=0, keepdims=True)
    middle = jnp.where(stage == 1, target_row, column)
    found = (owners == middle) & (cols == wanted)
    right = jnp.min(jnp.where(found, at, PANEL), axis=0, keepdims=True)

    def scalar(vector, q):
        return jnp.sum(jnp.where(lane == q, vector, 0))

    for j in range(ROWS):
        for a in range(SLOTS):
            index[j * SLOTS + a] = scalar(left, (j * SLOTS + a) * SLOTS)
    for q in range(QUERIES):
        index[CHUNKS + q] = scalar(right, q)


def split(value):
    high = value.astype(jnp.bfloat16)
    return high, (value - high.astype(jnp.float32)).astype(jnp.bfloat16)


def dot3(left, right_high, right_low):
    high, low = split(left)
    dot = functools.partial(jnp.dot, preferred_element_type=jnp.float32)
    return dot(high, right_high) + (dot(high, right_low) + dot(low, right_high))


def kernel(
    targets, blocks, labels, out, panel, known, right_high, right_low, index, send_sem, recv_sem, own_sem
):
    x, z_hi, core, y, z_lo = place()
    z = z_hi * Z_LO + z_lo

    def at(x_, z_, core_, y_):
        return ((x_ * 2 + z_ // Z_LO) * 2 + core_, y_ * Z_LO + z_ % Z_LO)

    def along_z(by):
        return at(x, (z + by + 2 * Z_LO) % (2 * Z_LO), core, y)

    inner_low = (z_lo + Z_LO - 1) // Z_LO
    edge_high = (z_lo + 1) // Z_LO
    edge_low = 1 - inner_low
    edge = edge_low + edge_high
    x_to = at((x + 5 - 2 * z_hi) % 4, z, core, y)
    x_from = at((x + 3 + 2 * z_hi) % 4, z, core, y)
    y_to = at(x, z, core, (y + 5 - 2 * edge_high) % 4)
    y_from = at(x, z, core, (y + 3 + 2 * edge_high) % 4)
    sibling = at(x, z, 1 - core, y)
    below, above = P7 + (YF - P7) * edge_low, P9 + (YF - P9) * edge_high

    for p in (YN, YF):
        known[p] = jnp.full(known.shape[1:], -2, jnp.int32)

    barrier = pltpu.get_barrier_semaphore()
    peers = [along_z(by) for by in (1, -1, 6, -6)] + [x_to, x_from, y_to, y_from, sibling]
    for peer in peers:
        pl.semaphore_signal(barrier, inc=1, device_id=peer, device_id_type=MESH)
    pl.semaphore_wait(barrier, len(peers))

    def part(i):
        return pl.ds(i % PARTS * (ORDER // PARTS), ORDER // PARTS)

    def ref(place_, i):
        if place_ is None:
            return labels if i == PIECES else blocks.at[i // PARTS, part(i)]
        return known.at[place_] if i == PIECES else panel.at[place_ * CHUNKS + i // PARTS, part(i)]

    def copy(src, dst, i, peer):
        return pltpu.make_async_remote_copy(
            src_ref=ref(src, i),
            dst_ref=ref(dst, i),
            send_sem=send_sem.at[dst, i],
            recv_sem=recv_sem.at[dst, i],
            device_id=peer,
            device_id_type=MESH,
        )

    def send(src, dst, i, peer):
        copy(src, dst, i, peer).start()

    def arrived(dst, i):
        copy(dst, dst, i, sibling).wait_recv()

    def sent(dst, i):
        copy(dst, dst, i, sibling).wait_send()

    steps = PIECES // 2
    pieces = list(range(PIECES + 1))
    upward = {i: i < steps or i == PIECES for i in pieces}

    def of(k):
        return ([PIECES] if k == 0 else []) + [k, k + steps]

    def start(k):
        for i in of(k):
            send(None, M1 if upward[i] else P1, i, along_z(1 if upward[i] else -1))

    def six_on(k):
        for i in of(k):
            here = M1 if upward[i] else P1
            arrived(here, i)
            send(None, P1 if upward[i] else M1, i, along_z(-1 if upward[i] else 1))
            send(here, P9 if upward[i] else P7, i, along_z(6 if upward[i] else -6))

            @pl.when(edge_low == 1 if upward[i] else edge_high == 1)
            def _():
                send(here, YF, i, y_to)

    def other_way(k):
        for i in of(k):
            here = P1 if upward[i] else M1
            arrived(here, i)

            @pl.when(edge_high == 1 if upward[i] else edge_low == 1)
            def _():
                send(here, YF, i, y_to)

    def near(k):
        for i in of(k):
            @pl.when(edge_low == 0)
            def _():
                send(M1, SB, i, sibling)

            @pl.when(edge_high == 0)
            def _():
                send(P1, SA, i, sibling)

    def to_far(k):
        for i in of(k):
            here = P9 if upward[i] else P7
            arrived(here, i)
            send(here, FC, i, along_z(1 if upward[i] else -1))

            @pl.when(edge_high == 1 if upward[i] else edge_low == 1)
            def _():
                send(here, YN, i, y_to)

    def cross(k):
        for i in of(k):
            @pl.when(edge == 1)
            def _():
                arrived(YF, i)

            if upward[i]:
                send(above, XA, i, x_to)
            else:
                send(below, XB, i, x_to)

    def past_far(k):
        for i in of(k):
            arrived(FC, i)
            send(FC, P7 if upward[i] else P9, i, along_z(1 if upward[i] else -1))
            send(FC, XC, i, x_to)

    def end(k):
        for i in of(k):
            here = P7 if upward[i] else P9
            arrived(here, i)
            if upward[i]:
                send(below, XB, i, x_to)
            else:
                send(above, XA, i, x_to)

            @pl.when(edge_low == 1 if upward[i] else edge_high == 1)
            def _():
                send(here, YN, i, y_to)

    crossed = (z_hi + core) % 2
    pass_center = FC + (XC - FC) * crossed
    pass_below = below + (XB - below) * crossed
    pass_above = above + (XA - above) * crossed

    def pass_on(k, early):
        for i in of(k):
            if upward[i] == early:
                arrived(XA, i)
                send(pass_above, TA, i, sibling)
            else:
                arrived(XB, i)
                send(pass_below, TB, i, sibling)

    def pass_far(k):
        for i in of(k):
            arrived(XC, i)
            send(pass_center, TC, i, sibling)

    def near_end(which):
        @pl.when(edge_low == 1)
        def _():
            for i in which:
                arrived(YN, i)
                send(YN, SB, i, sibling)

        @pl.when(edge_high == 1)
        def _():
            for i in which:
                arrived(YN, i)
                send(YN, SA, i, sibling)

    for k in range(steps):
        start(k)
    for k in range(steps):
        for i in of(k):
            send(None, SC, i, sibling)
    own = PLACES * CHUNKS
    mine = pltpu.make_async_copy(blocks, panel.at[pl.ds(own, CHUNKS)], own_sem)
    mine.start()
    panel[PANEL] = jnp.zeros((ORDER, ORDER), jnp.float32)
    known[PLACES] = labels[...]

    def at_step(k, work):
        if 0 <= k < steps:
            work(k)

    core_places = (SC, SB, SA, TC, TB, TA)
    for k in range(AHEAD):
        six_on(k)
    for k in range(steps + 4):
        at_step(k, other_way)
        at_step(k, to_far)
        at_step(k - 1, past_far)
        at_step(k + AHEAD, six_on)
        at_step(k, cross)
        at_step(k - 2, end)
        at_step(k, near)
        at_step(k - 2, lambda k: pass_on(k, True))
        at_step(k - 3, pass_far)
        at_step(k - 4, lambda k: near_end(of(k)))
        at_step(k - 4, lambda k: pass_on(k, False))
        if k == steps + 1:
            for p in core_places:
                arrived(p, PIECES)
            find(targets, known, index)
    for i in pieces[:-1]:
        for p in core_places:
            arrived(p, i)

    mine.wait()

    def product(stage, j, left):
        for a in range(SLOTS):
            for b in range(SLOTS):
                at_ = index[CHUNKS + ((stage * ROWS + j) * SLOTS + a) * SLOTS + b]
                rows, cols = pl.ds(a * ORDER, ORDER), pl.ds(b * ORDER, ORDER)
                high, low = split(panel[at_])
                right_high[rows, cols] = high
                right_low[rows, cols] = low
        return dot3(left, right_high[...], right_low[...])

    for j in range(ROWS):
        left = jnp.concatenate([panel[index[j * SLOTS + a]] for a in range(SLOTS)], axis=1)
        square = product(0, j, left)
        cube = product(1, j, square)
        result = 3.0 * square - 2.0 * cube
        for b in range(SLOTS):
            out[j, b] = result[:, b * ORDER : (b + 1) * ORDER]

    always = [p for p in range(PLACES) if p not in (YN, YF)]
    for i in pieces:
        for p in always:
            sent(p, i)

    @pl.when(edge == 1)
    def _():
        for i in pieces:
            sent(YN, i)
            sent(YF, i)


def per_device(blocks, columns, owner_map, targets):
    def lanes(values):
        return jnp.broadcast_to(values.reshape(-1, 1), (CHUNKS, 128))

    labels = jnp.concatenate([lanes(jnp.repeat(owner_map, SLOTS)), lanes(columns)], axis=0)
    vmem = pl.BlockSpec(memory_space=pltpu.VMEM)
    return pl.pallas_call(
        kernel,
        out_shape=jax.ShapeDtypeStruct((ROWS, SLOTS, ORDER, ORDER), jnp.float32),
        in_specs=[
            pl.BlockSpec(memory_space=pltpu.SMEM),
            pl.BlockSpec(memory_space=pl.ANY),
            vmem,
        ],
        out_specs=vmem,
        scratch_shapes=[
            pltpu.VMEM((PANEL + 1, ORDER, ORDER), jnp.float32),
            pltpu.VMEM((PLACES + 1, 2 * CHUNKS, 128), jnp.int32),
            pltpu.VMEM((SLOTS * ORDER, SLOTS * ORDER), jnp.bfloat16),
            pltpu.VMEM((SLOTS * ORDER, SLOTS * ORDER), jnp.bfloat16),
            pltpu.SMEM((CHUNKS + QUERIES,), jnp.int32),
            pltpu.SemaphoreType.DMA((PLACES, PIECES + 1)),
            pltpu.SemaphoreType.DMA((PLACES, PIECES + 1)),
            pltpu.SemaphoreType.DMA,
        ],
        compiler_params=pltpu.CompilerParams(collective_id=0, has_side_effects=True),
        name="purify",
    )(targets, blocks.reshape(CHUNKS, ORDER, ORDER), labels)


def solution(mesh):
    return jax.shard_map(
        per_device,
        mesh=mesh,
        in_specs=(
            P(("blk", "grp"), None, None, None),
            P(("blk", "grp"), None),
            P(("blk", "grp")),
            P(("blk", "grp"), None),
        ),
        out_specs=P(("blk", "grp"), None, None, None),
        check_vma=False,
    )
```
